32 devices in a mesh: row: 8 (over z, x), col: 4 (over y, core).
Axes of the slice: x: 2, y: 2, z: 4, core: 2. Of those that a mesh axis runs over, the one named last changes fastest.
Arguments:
- diagonal_inverses: bfloat16 [24, 2048, 2048], P('row', 'col'), may hold values from -0.125 to 0.125
- column_basis: bfloat16 [24, 2048, 256], P('row', 'col'), may hold values from -6 to 6
- row_basis: bfloat16 [24, 2048, 256], P('row', 'col'), may hold values from -0.125 to 0.125
- transfer: float32 [24, 256, 256], P('row', 'col'), may hold values from -0.375 to 0.375
- coupling: float32 [24, 256, 256], P('row', 'col'), may hold values from -6 to 6
- ranks: int32 [24], P('row'), may hold values from 128 to 256, as said below
Outputs:
- merged: float32 [24, 256, 256], P('row', 'col')
- parent_skeleton: float32 [24, 256, 256], P('row', 'col')
The draws below stay inside these ranges and needn't reach their ends.
Inputs may be any that keep to these rules, and one draw needn't show every extreme that they name: `ranks`: each rank is 128 or 256; both occur in every draw.
All inputs are finite; a program needn't handle non-finite values.
Results may differ from the reference program's by a relative error of at most 0.0021.
Values may be sent and summed in bfloat16 or wider, within the bound.
A program may use at most 64 MiB of HBM per device.

```python
import jax
import jax.numpy as jnp
from jax import lax

M = 2048
R = 256
NODE_DEV = 3
BIT = 2
NODES = 24


def draw_ranks(key, part):
    picked = jax.random.randint(key, (NODES,), 1, 3)
    picked = picked.at[0].set(2).at[1].set(1)
    return (picked * (R // 2)).astype(jnp.int32)


def block_levels(key, extent, shards, smallest, top_value):
    def one(axis_at, shards_of):
        steps = jax.random.uniform(jax.random.fold_in(jax.random.fold_in(key, 6), axis_at), (shards_of,), jnp.float32, smallest / len(shards), top_value / len(shards))
        return jnp.repeat(jnp.exp(steps), extent[axis_at] // shards_of).reshape((-1,) + (1,) * (len(extent) - axis_at - 1))

    loudness = one(*shards[0])
    for cut in shards[1:]:
        loudness = loudness * one(*cut)
    return loudness


def normal_values(key, shape, width, most, split=(), kind=jnp.bfloat16):
    values = jax.random.normal(key, shape, jnp.float32) * width
    if len(split) > 0:
        values = block_levels(key, shape, split, -0.22, 0.18) * values
    return jnp.clip(values, min=-most, max=most).astype(kind)


def setup_inputs(seed: int = 0) -> dict:
    keys = jax.random.split(jax.random.key(seed), 7)
    return {
        "diagonal_inverses": normal_values(keys[0], (NODES, M, M), M ** -0.5, 0.125, ((0, 8), (1, 4))),
        "column_basis": normal_values(keys[1], (NODES, M, R), 1.0, 6.0, ((0, 8), (1, 4))),
        "row_basis": normal_values(keys[2], (NODES, M, R), M ** -0.5, 0.125, ((0, 8), (1, 4))),
        "transfer": normal_values(keys[3], (NODES, R, R), R ** -0.5, 0.375, ((0, 8), (1, 4)), jnp.float32),
        "coupling": normal_values(keys[4], (NODES, R, R), 1.0, 6.0, ((0, 8), (1, 4)), jnp.float32),
        "ranks": draw_ranks(jax.random.fold_in(keys[6], 71), 0),
    }


def leaf_skeleton(items):
    block_entry, left_factor_basis, right_factor_basis, live_cols = items
    left_factor_basis = jnp.where(live_cols[None, :], left_factor_basis, jnp.zeros_like(left_factor_basis))
    right_factor_basis = jnp.where(live_cols[None, :], right_factor_basis, jnp.zeros_like(right_factor_basis))
    eliminated_part = jnp.dot(block_entry, left_factor_basis, preferred_element_type=jnp.float32).astype(jnp.bfloat16)
    return jnp.dot(right_factor_basis.T, eliminated_part, preferred_element_type=jnp.float32)


def reference(diagonal_inverses, column_basis, row_basis, transfer, coupling, ranks):
    node_count = transfer.shape[0]
    rank_width = transfer.shape[1]
    live_cols = jnp.arange(rank_width, dtype=jnp.int32)[None, :] < ranks[:, None]
    skeleton = lax.map(leaf_skeleton, (diagonal_inverses, column_basis, row_basis, live_cols))
    masked = transfer * live_cols[:, :, None].astype(jnp.float32)
    node_ids = jnp.arange(node_count, dtype=jnp.int32)
    sibling = jnp.bitwise_xor(node_ids // NODE_DEV, 2 ** BIT) * NODE_DEV + node_ids % NODE_DEV
    masked_sib = masked[sibling]
    highest = lax.Precision.HIGHEST
    merged = jnp.einsum('nij,njk->nik', skeleton, masked, precision=highest)
    merged = merged + jnp.einsum('nij,njk->nik', coupling, masked_sib, precision=highest)
    parent = jnp.einsum('nji,njk->nik', masked, merged, precision=highest)
    parent = parent + jnp.einsum('nji,njk->nik', masked_sib, merged[sibling], precision=highest)
    return merged, parent
```

```python
import jax
import jax.numpy as jnp
from jax import lax
from jax.experimental import pallas as pl
from jax.experimental.pallas import tpu as pltpu
from jax.sharding import PartitionSpec as P

BIT = 2
MESH = pl.DeviceIdType.MESH
LY, LC, LF, TY, TC, TF, TZ, TG, ZC, ZG, SC, SY, PC, PY, PZ = range(15)


def kernel(
    ranks_ref, d_ref, l_ref, r_ref, t_ref, k_ref, merged_ref, parent_ref,
    dv, lv, rv, tv, kv, tw, zw, sbuf, sgot, ysend, ygot, pbuf, pgot, pysend, pygot,
    esend, egot, mv, pv, send_sem, recv_sem, d_sem, loc_sem, out_sem,
):
    nodes, block, _ = l_ref.shape
    part = t_ref.shape[1]
    width = t_ref.shape[2]
    highest = lax.Precision.HIGHEST
    c = lax.axis_index("col")
    r = lax.axis_index("row")
    core = lax.rem(c, 2)
    y = lax.div(c, 2)
    cp = c + 1 - 2 * core
    yp = c + 2 - 4 * y
    high = lax.rem(lax.div(r, 1 << BIT), 2)
    sib = r + (1 << BIT) - (2 << BIT) * high
    other = 1 - y

    to_core = {"col": cp}
    to_y = {"col": yp}
    to_z = {"row": sib}
    slots = (c, cp, yp, cp + yp - c)

    def rows_of(index):
        return pl.ds(pl.multiple_of(index * part, part), part)

    t_in = pltpu.make_async_copy(t_ref, tv, loc_sem.at[0])
    t_in.start()
    l_in, d_in = [], []
    for n in range(nodes):
        cp_l = pltpu.make_async_copy(l_ref.at[n], lv.at[n, pl.ds(0, block)], d_sem.at[n, 4])
        cp_l.start()
        l_in.append(cp_l)
        for s in range(4):
            src = d_ref.at[n, :, pl.ds(pl.multiple_of(slots[s] * block, block), block)]
            one = pltpu.make_async_copy(src, dv.at[n, :, pl.ds(s * block, block)], d_sem.at[n, s])
            one.start()
            d_in.append(one)
    r_in = pltpu.make_async_copy(r_ref, rv, loc_sem.at[1])
    r_in.start()
    k_in = pltpu.make_async_copy(k_ref, kv, loc_sem.at[2])
    k_in.start()

    barrier = pltpu.get_barrier_semaphore()
    for device in (to_core, to_y, to_z):
        pl.semaphore_signal(barrier, inc=1, device_id=device, device_id_type=MESH)

    t_in.wait()
    row_at = lax.broadcasted_iota(jnp.int32, (part, width), 0) + c * part
    col_at = lax.broadcasted_iota(jnp.int32, (part, width), 1)
    for n in range(nodes):
        tw[n, rows_of(c), :] = jnp.where(row_at < ranks_ref[n], tv[n], 0.0)
    pl.semaphore_wait(barrier, 3)

    sent = []

    def copy(kind, n, src, dst, device):
        return pltpu.make_async_remote_copy(
            src_ref=src, dst_ref=dst, send_sem=send_sem.at[kind, n], recv_sem=recv_sem.at[kind, n],
            device_id=device, device_id_type=MESH,
        )

    def send(kind, n, src, dst, device):
        one = copy(kind, n, src, dst, device)
        one.start()
        sent.append(one)

    def got(kind, n, ref, device):
        copy(kind, n, ref, ref, device).wait_recv()

    def slot(n, s):
        return lv.at[n, pl.ds(s * block, block)]

    def strip(buf, n, index):
        return buf.at[n, rows_of(index)]

    for n in range(nodes):
        send(TY, n, strip(tw, n, c), strip(tw, n, c), to_y)
        send(LY, n, l_ref.at[n], slot(n, 2), to_y)
        send(LC, n, l_ref.at[n], slot(n, 1), to_core)
        send(TZ, n, strip(tw, n, c), strip(zw, n, c), to_z)
        send(TC, n, strip(tw, n, c), strip(tw, n, c), to_core)

    def times(n, first, count):
        span = pl.ds(first * block, count * block)
        return jnp.dot(dv[n, :, span], lv[n, span, :], preferred_element_type=jnp.float32)

    def eliminate(n):
        got(TY, n, strip(tw, n, yp), to_y)
        send(TG, n, strip(tw, n, yp), strip(zw, n, yp), to_z)
        send(TF, n, strip(tw, n, yp), strip(tw, n, yp), to_core)
        l_in[n].wait()
        for s in range(4):
            d_in[4 * n + s].wait()
        got(LC, n, slot(n, 1), to_core)
        total = times(n, 0, 2)
        got(LY, n, slot(n, 2), to_y)
        send(LF, n, slot(n, 2), slot(n, 3), to_core)
        total = total + times(n, 2, 1)
        got(LF, n, slot(n, 3), to_core)
        total = total + times(n, 3, 1)
        skeleton = lax.dot_general(
            rv[n], total.astype(jnp.bfloat16), (((0,), (0,)), ((), ())), preferred_element_type=jnp.float32
        )
        sbuf[n] = skeleton.reshape(2, 2, part, width)
        send(SC, n, sbuf.at[n, :, 1 - core], sgot.at[n], to_core)

    def reduce_chip(n):
        got(SC, n, sgot.at[n], to_core)
        ysend[n] = (sbuf[n, other, core] + sgot[n, other]).astype(ysend.dtype)
        send(SY, n, ysend.at[n], ygot.at[n], to_y)

    def hand_on_sibling(n):
        got(TZ, n, strip(zw, n, c), to_z)
        send(ZC, n, strip(zw, n, c), strip(zw, n, c), to_core)
        got(TG, n, strip(zw, n, yp), to_z)
        send(ZG, n, strip(zw, n, yp), strip(zw, n, yp), to_core)

    def couple(n):
        got(ZC, n, strip(zw, n, cp), to_core)
        got(ZG, n, strip(zw, n, slots[3]), to_core)
        got(TC, n, strip(tw, n, cp), to_core)
        got(TF, n, strip(tw, n, slots[3]), to_core)
        mv[n] = jnp.dot(kv[n], zw[n], precision=highest, preferred_element_type=jnp.float32)

    outs = []

    def merge(n):
        got(SY, n, ygot.at[n], to_y)
        mine = sbuf[n, y, core] + sgot[n, y] + ygot[n].astype(jnp.float32)
        live = (row_at < ranks_ref[n]) & (col_at < ranks_ref[n])
        mine = jnp.where(live, mine, 0.0)
        merged = mv[n] + jnp.dot(mine, tw[n], precision=highest, preferred_element_type=jnp.float32)
        mv[n] = merged
        own = lax.dot_general(
            tw[n, rows_of(c), :], merged, (((0,), (0,)), ((), ())), precision=highest,
            preferred_element_type=jnp.float32,
        )
        pbuf[n] = own.reshape(2, 2, part, width)
        send(PC, n, pbuf.at[n, :, 1 - core], pgot.at[n], to_core)
        one = pltpu.make_async_copy(mv.at[n], merged_ref.at[n], out_sem.at[0, n])
        one.start()
        outs.append(one)

    def parent_chip(n):
        got(PC, n, pgot.at[n], to_core)
        pysend[n] = (pbuf[n, other, core] + pgot[n, other]).astype(pysend.dtype)
        send(PY, n, pysend.at[n], pygot.at[n], to_y)

    def parent_own(n):
        got(PY, n, pygot.at[n], to_y)
        own = pbuf[n, y, core] + pgot[n, y] + pygot[n].astype(jnp.float32)
        pv[n] = own
        esend[n] = own.astype(esend.dtype)
        send(PZ, n, esend.at[n], egot.at[n], to_z)

    def parent_all(n):
        got(PZ, n, egot.at[n], to_z)
        pv[n] = pv[n] + egot[n].astype(jnp.float32)
        one = pltpu.make_async_copy(pv.at[n], parent_ref.at[n], out_sem.at[1, n])
        one.start()
        outs.append(one)

    r_in.wait()
    for n in range(nodes):
        eliminate(n)
        if n >= 1:
            reduce_chip(n - 1)
            hand_on_sibling(n - 1)
    k_in.wait()
    hand_on_sibling(nodes - 1)
    for n in range(nodes - 1):
        couple(n)
    reduce_chip(nodes - 1)
    couple(nodes - 1)
    for n in range(nodes):
        merge(n)
        if n >= 1:
            parent_chip(n - 1)
    for n in range(nodes - 1):
        parent_own(n)
    parent_chip(nodes - 1)
    for n in range(nodes - 1):
        parent_all(n)
    parent_own(nodes - 1)
    parent_all(nodes - 1)
    for one in sent:
        one.wait_send()
    for one in outs:
        one.wait()


def shards(diagonal_inverses, column_basis, row_basis, transfer, coupling, ranks):
    nodes, block, whole = diagonal_inverses.shape
    part, width = transfer.shape[1:]
    f32, bf16 = jnp.float32, jnp.bfloat16
    skeleton_link, parent_link, sibling_link = f32, f32, f32
    anywhere = pl.BlockSpec(memory_space=pl.ANY)
    strips = (nodes, part, width)
    square = (nodes, width, width)
    quads = (nodes, 2, 2, part, width)
    pairs = (nodes, 2, part, width)
    shape = jax.ShapeDtypeStruct(strips, f32)
    return pl.pallas_call(
        kernel,
        out_shape=(shape, shape),
        in_specs=[pl.BlockSpec(memory_space=pltpu.SMEM)] + [anywhere] * 5,
        out_specs=(anywhere, anywhere),
        scratch_shapes=[
            pltpu.VMEM((nodes, block, whole), bf16),
            pltpu.VMEM((nodes, whole, width), bf16),
            pltpu.VMEM((nodes, block, width), bf16),
            pltpu.VMEM(strips, f32),
            pltpu.VMEM(strips, f32),
            pltpu.VMEM(square, f32),
            pltpu.VMEM(square, f32),
            pltpu.VMEM(quads, f32),
            pltpu.VMEM(pairs, f32),
            pltpu.VMEM(strips, skeleton_link),
            pltpu.VMEM(strips, skeleton_link),
            pltpu.VMEM(quads, f32),
            pltpu.VMEM(pairs, f32),
            pltpu.VMEM(strips, parent_link),
            pltpu.VMEM(strips, parent_link),
            pltpu.VMEM(strips, sibling_link),
            pltpu.VMEM(strips, sibling_link),
            pltpu.VMEM(strips, f32),
            pltpu.VMEM(strips, f32),
            pltpu.SemaphoreType.DMA((15, nodes)),
            pltpu.SemaphoreType.DMA((15, nodes)),
            pltpu.SemaphoreType.DMA((nodes, 5)),
            pltpu.SemaphoreType.DMA((3,)),
            pltpu.SemaphoreType.DMA((2, nodes)),
        ],
        compiler_params=pltpu.CompilerParams(collective_id=0, has_side_effects=True),
    )(ranks, diagonal_inverses, column_basis, row_basis, transfer, coupling)


def solution(mesh):
    placed = (P("row", "col", None),) * 5 + (P("row"),)
    return jax.shard_map(
        shards,
        mesh=mesh,
        in_specs=placed,
        out_specs=(P("row", "col", None), P("row", "col", None)),
        check_vma=False,
    )
```

```python
import jax
import jax.numpy as jnp
from jax import lax
from jax.experimental import pallas as pl
from jax.experimental.pallas import tpu as pltpu
from jax.sharding import PartitionSpec as P

BIT = 2
MESH = pl.DeviceIdType.MESH
LY, LC, LF, TY, TC, TF, TZ, TG, ZC, ZG, SC, SY, PC, PY, PZ, MY, MF = range(17)


def kernel(
    ranks_ref, d_ref, l_ref, r_ref, t_ref, k_ref, merged_ref, parent_ref,
    dv, lv, rv, tv, kv, tw, zw, sbuf, sgot, ysend, ygot, pbuf, pgot, pysend, pygot,
    esend, egot, mv, pv, send_sem, recv_sem, d_sem, loc_sem, out_sem,
):
    nodes, block, _ = l_ref.shape
    part = t_ref.shape[1]
    width = t_ref.shape[2]
    c = lax.axis_index("col")
    r = lax.axis_index("row")
    core = lax.rem(c, 2)
    y = lax.div(c, 2)
    cp = c + 1 - 2 * core
    yp = c + 2 - 4 * y
    high = lax.rem(lax.div(r, 1 << BIT), 2)
    sib = r + (1 << BIT) - (2 << BIT) * high
    other = 1 - y

    to_core = {"col": cp}
    to_y = {"col": yp}
    to_z = {"row": sib}
    slots = (c, cp, yp, cp + yp - c)

    def halves(x):
        top = x.astype(jnp.bfloat16)
        return top, (x - top.astype(jnp.float32)).astype(jnp.bfloat16)

    def product(a, b, dims):
        a_top, a_low = halves(a)
        b_top, b_low = halves(b)
        lhs = jnp.concatenate([a_top, a_low, a_top], axis=dims[0])
        rhs = jnp.concatenate([b_top, b_top, b_low], axis=dims[1])
        return lax.dot_general(
            lhs, rhs, (((dims[0],), (dims[1],)), ((), ())), preferred_element_type=jnp.float32
        )

    def rows_of(index):
        return pl.ds(pl.multiple_of(index * part, part), part)

    t_in = pltpu.make_async_copy(t_ref, tv, loc_sem.at[0])
    t_in.start()
    barrier = pltpu.get_barrier_semaphore()
    for device in (to_core, to_y, to_z):
        pl.semaphore_signal(barrier, inc=1, device_id=device, device_id_type=MESH)

    row_at = lax.broadcasted_iota(jnp.int32, (part, width), 0) + c * part
    col_at = lax.broadcasted_iota(jnp.int32, (part, width), 1)
    pl.semaphore_wait(barrier, 3)

    sent = []

    def copy(kind, n, src, dst, device):
        return pltpu.make_async_remote_copy(
            src_ref=src, dst_ref=dst, send_sem=send_sem.at[kind, n], recv_sem=recv_sem.at[kind, n],
            device_id=device, device_id_type=MESH,
        )

    def send(kind, n, src, dst, device):
        one = copy(kind, n, src, dst, device)
        one.start()
        sent.append(one)

    def got(kind, n, ref, device):
        copy(kind, n, ref, ref, device).wait_recv()

    def slot(n, s):
        return lv.at[n, pl.ds(s * block, block)]

    def strip(buf, n, index):
        return buf.at[n, rows_of(index)]

    half = block // 2
    last = nodes - 1

    def piece(n, s, first):
        return lv.at[n, pl.ds(s * block + first, half)]

    def send_basis(n):
        send(LY, n, l_ref.at[n], slot(n, 2), to_y)

    send_basis(0)
    send(LC, 0, l_ref.at[0], slot(0, 1), to_core)
    t_in.wait()
    for n in range(nodes):
        tw[n, rows_of(c), :] = jnp.where(row_at < ranks_ref[n], tv[n], 0.0)
    for n in range(nodes):
        send(TY, n, strip(tw, n, c), strip(tw, n, c), to_y)
        send(TZ, n, strip(tw, n, c), strip(zw, n, c), to_z)
        send(TC, n, strip(tw, n, c), strip(tw, n, c), to_core)
    for n in range(1, nodes - 1):
        send_basis(n)
    l_in, d_in = [], []
    for n in range(nodes):
        cp_l = pltpu.make_async_copy(l_ref.at[n], lv.at[n, pl.ds(0, block)], d_sem.at[n, 4])
        cp_l.start()
        l_in.append(cp_l)
        if n >= 1:
            send(LC, n, l_ref.at[n], slot(n, 1), to_core)
        for s in range(4):
            src = d_ref.at[n, :, pl.ds(pl.multiple_of(slots[s] * block, block), block)]
            one = pltpu.make_async_copy(src, dv.at[n, :, pl.ds(s * block, block)], d_sem.at[n, s])
            one.start()
            d_in.append(one)
    r_in = pltpu.make_async_copy(r_ref, rv, loc_sem.at[1])
    r_in.start()
    k_in = pltpu.make_async_copy(k_ref, kv, loc_sem.at[2])
    k_in.start()


    def times(n, first, size):
        span = pl.ds(first, size)
        return jnp.dot(dv[n, :, span], lv[n, span, :], preferred_element_type=jnp.float32)

    def relay(n):
        got(TY, n, strip(tw, n, yp), to_y)
        send(TG, n, strip(tw, n, yp), strip(zw, n, yp), to_z)
        send(TF, n, strip(tw, n, yp), strip(tw, n, yp), to_core)

    def begin(n):
        l_in[n].wait()
        for s in range(4):
            d_in[4 * n + s].wait()
        got(LC, n, slot(n, 1), to_core)
        return times(n, 0, 2 * block)

    def eliminate(n):
        total = begin(n)
        got(LY, n, slot(n, 2), to_y)
        send(LF, n, slot(n, 2), slot(n, 3), to_core)
        total = total + times(n, 2 * block, block)
        got(LF, n, slot(n, 3), to_core)
        total = total + times(n, 3 * block, block)
        skeletons(n, total)

    def skeletons(n, total):
        skeleton = lax.dot_general(
            rv[n], total.astype(jnp.bfloat16), (((0,), (0,)), ((), ())), preferred_element_type=jnp.float32
        )
        sbuf[n] = skeleton.reshape(2, 2, part, width)
        send(SC, n, sbuf.at[n, :, 1 - core], sgot.at[n], to_core)

    def reduce_chip(n):
        got(SC, n, sgot.at[n], to_core)
        ysend[n] = (sbuf[n, other, core] + sgot[n, other]).astype(ysend.dtype)
        send(SY, n, ysend.at[n], ygot.at[n], to_y)

    def hand_on_sibling(n):
        got(TZ, n, strip(zw, n, c), to_z)
        send(ZC, n, strip(zw, n, c), strip(zw, n, c), to_core)
        got(TG, n, strip(zw, n, yp), to_z)
        send(ZG, n, strip(zw, n, yp), strip(zw, n, yp), to_core)

    def couple(n):
        got(ZC, n, strip(zw, n, cp), to_core)
        got(ZG, n, strip(zw, n, slots[3]), to_core)
        got(TC, n, strip(tw, n, cp), to_core)
        got(TF, n, strip(tw, n, slots[3]), to_core)
        mv[n] = product(kv[n], zw[n], (1, 0))

    outs = []

    def merge(n):
        got(SY, n, ygot.at[n], to_y)
        mine = sbuf[n, y, core] + sgot[n, y] + ygot[n].astype(jnp.float32)
        live = (row_at < ranks_ref[n]) & (col_at < ranks_ref[n])
        mine = jnp.where(live, mine, 0.0)
        merged = mv[n] + product(mine, tw[n], (1, 0))
        mv[n] = merged
        own = product(tw[n, rows_of(c), :], merged, (0, 0))
        pbuf[n] = own.reshape(2, 2, part, width)
        send(PC, n, pbuf.at[n, :, 1 - core], pgot.at[n], to_core)
        one = pltpu.make_async_copy(mv.at[n], merged_ref.at[n], out_sem.at[0, n])
        one.start()
        outs.append(one)

    def parent_chip(n):
        got(PC, n, pgot.at[n], to_core)
        pysend[n] = (pbuf[n, other, core] + pgot[n, other]).astype(pysend.dtype)
        send(PY, n, pysend.at[n], pygot.at[n], to_y)

    def parent_own(n):
        got(PY, n, pygot.at[n], to_y)
        own = pbuf[n, y, core] + pgot[n, y] + pygot[n].astype(jnp.float32)
        pv[n] = own
        esend[n] = own.astype(esend.dtype)
        send(PZ, n, esend.at[n], egot.at[n], to_z)

    def parent_all(n):
        got(PZ, n, egot.at[n], to_z)
        pv[n] = pv[n] + egot[n].astype(jnp.float32)
        one = pltpu.make_async_copy(pv.at[n], parent_ref.at[n], out_sem.at[1, n])
        one.start()
        outs.append(one)

    r_in.wait()
    k_in.wait()
    eliminate(0)
    for n in range(nodes):
        relay(n)
    reduce_chip(0)
    send(LY, last, l_ref.at[last, pl.ds(0, half)], piece(last, 2, 0), to_y)
    for n in range(nodes):
        got(TZ, n, strip(zw, n, c), to_z)
        send(ZC, n, strip(zw, n, c), strip(zw, n, c), to_core)
    for n in range(1, last):
        eliminate(n)
        reduce_chip(n)
    send(MY, last, l_ref.at[last, pl.ds(half, half)], piece(last, 2, half), to_y)

    def hand_on(n):
        got(TG, n, strip(zw, n, yp), to_z)
        send(ZG, n, strip(zw, n, yp), strip(zw, n, yp), to_core)

    hand_on(0)
    couple(0)
    merge(0)
    total = begin(last)
    parent_chip(0)
    for n in range(1, last):
        hand_on(n)
    got(LY, last, piece(last, 2, 0), to_y)
    send(LF, last, piece(last, 2, 0), piece(last, 3, 0), to_core)
    total = total + times(last, 2 * block, half)
    for n in range(1, last):
        couple(n)
        merge(n)
        parent_chip(n)
    got(LF, last, piece(last, 3, 0), to_core)
    total = total + times(last, 3 * block, half)
    got(MY, last, piece(last, 2, half), to_y)
    send(MF, last, piece(last, 2, half), piece(last, 3, half), to_core)
    total = total + times(last, 2 * block + half, half)
    got(MF, last, piece(last, 3, half), to_core)
    total = total + times(last, 3 * block + half, half)
    skeletons(last, total)
    hand_on(last)
    reduce_chip(last)
    couple(last)
    for n in range(last):
        parent_own(n)
    merge(last)
    parent_chip(last)
    for n in range(last):
        parent_all(n)
    parent_own(last)
    parent_all(last)
    for one in sent:
        one.wait_send()
    for one in outs:
        one.wait()


def shards(diagonal_inverses, column_basis, row_basis, transfer, coupling, ranks):
    nodes, block, whole = diagonal_inverses.shape
    part, width = transfer.shape[1:]
    f32, bf16 = jnp.float32, jnp.bfloat16
    skeleton_link, parent_link, sibling_link = bf16, bf16, f32
    anywhere = pl.BlockSpec(memory_space=pl.ANY)
    strips = (nodes, part, width)
    square = (nodes, width, width)
    quads = (nodes, 2, 2, part, width)
    pairs = (nodes, 2, part, width)
    shape = jax.ShapeDtypeStruct(strips, f32)
    return pl.pallas_call(
        kernel,
        out_shape=(shape, shape),
        in_specs=[pl.BlockSpec(memory_space=pltpu.SMEM)] + [anywhere] * 5,
        out_specs=(anywhere, anywhere),
        scratch_shapes=[
            pltpu.VMEM((nodes, block, whole), bf16),
            pltpu.VMEM((nodes, whole, width), bf16),
            pltpu.VMEM((nodes, block, width), bf16),
            pltpu.VMEM(strips, f32),
            pltpu.VMEM(strips, f32),
            pltpu.VMEM(square, f32),
            pltpu.VMEM(square, f32),
            pltpu.VMEM(quads, f32),
            pltpu.VMEM(pairs, f32),
            pltpu.VMEM(strips, skeleton_link),
            pltpu.VMEM(strips, skeleton_link),
            pltpu.VMEM(quads, f32),
            pltpu.VMEM(pairs, f32),
            pltpu.VMEM(strips, parent_link),
            pltpu.VMEM(strips, parent_link),
            pltpu.VMEM(strips, sibling_link),
            pltpu.VMEM(strips, sibling_link),
            pltpu.VMEM(strips, f32),
            pltpu.VMEM(strips, f32),
            pltpu.SemaphoreType.DMA((17, nodes)),
            pltpu.SemaphoreType.DMA((17, nodes)),
            pltpu.SemaphoreType.DMA((nodes, 5)),
            pltpu.SemaphoreType.DMA((3,)),
            pltpu.SemaphoreType.DMA((2, nodes)),
        ],
        compiler_params=pltpu.CompilerParams(collective_id=0, has_side_effects=True),
    )(ranks, diagonal_inverses, column_basis, row_basis, transfer, coupling)


def solution(mesh):
    placed = (P("row", "col", None),) * 5 + (P("row"),)
    return jax.shard_map(
        shards,
        mesh=mesh,
        in_specs=placed,
        out_specs=(P("row", "col", None), P("row", "col", None)),
        check_vma=False,
    )
```

```python
import jax
import jax.numpy as jnp
from jax import lax
from jax.experimental import pallas as pl
from jax.experimental.pallas import tpu as pltpu
from jax.sharding import PartitionSpec as P

BIT = 2
MESH = pl.DeviceIdType.MESH
LY, LC, LF, TY, TC, TF, TZ, TG, ZC, ZG, SC, SY, PC, PY, PZ, MY, MF = range(17)


def kernel(
    ranks_ref, d_ref, l_ref, r_ref, t_ref, k_ref, out_ref,
    dv, lv, rv, tv, kv, tw, zw, sbuf, sgot, ysend, ygot, pbuf, pgot, pysend, pygot, qsend, qgot,
    esend, egot, mv, pv, send_sem, recv_sem, d_sem, loc_sem, out_sem,
):
    nodes, block, _ = l_ref.shape
    part = t_ref.shape[1]
    width = t_ref.shape[2]
    c = lax.axis_index("col")
    r = lax.axis_index("row")
    core = lax.rem(c, 2)
    y = lax.div(c, 2)
    cp = c + 1 - 2 * core
    yp = c + 2 - 4 * y
    high = lax.rem(lax.div(r, 1 << BIT), 2)
    sib = r + (1 << BIT) - (2 << BIT) * high
    other = 1 - y

    to_core = {"col": cp}
    to_y = {"col": yp}
    to_z = {"row": sib}
    slots = (c, cp, yp, cp + yp - c)

    def halves(x):
        top = x.astype(jnp.bfloat16)
        return top, (x - top.astype(jnp.float32)).astype(jnp.bfloat16)

    def product(a, b, dims):
        a_top, a_low = halves(a)
        b_top, b_low = halves(b)
        lhs = jnp.concatenate([a_top, a_low, a_top], axis=dims[0])
        rhs = jnp.concatenate([b_top, b_top, b_low], axis=dims[1])
        return lax.dot_general(
            lhs, rhs, (((dims[0],), (dims[1],)), ((), ())), preferred_element_type=jnp.float32
        )

    def rows_of(index):
        return pl.ds(pl.multiple_of(index * part, part), part)

    t_in = pltpu.make_async_copy(t_ref, tv, loc_sem.at[0])
    t_in.start()
    barrier = pltpu.get_barrier_semaphore()
    for device in (to_core, to_y, to_z):
        pl.semaphore_signal(barrier, inc=1, device_id=device, device_id_type=MESH)

    row_at = lax.broadcasted_iota(jnp.int32, (part, width), 0) + c * part
    col_at = lax.broadcasted_iota(jnp.int32, (part, width), 1)
    l_in, d_in = [], []
    for n in range(nodes):
        cp_l = pltpu.make_async_copy(l_ref.at[n], lv.at[n, pl.ds(0, block)], d_sem.at[n, 4])
        cp_l.start()
        l_in.append(cp_l)
        for s in range(4):
            src = d_ref.at[n, :, pl.ds(pl.multiple_of(slots[s] * block, block), block)]
            one = pltpu.make_async_copy(src, dv.at[n, :, pl.ds(s * block, block)], d_sem.at[n, s])
            one.start()
            d_in.append(one)
    r_in = pltpu.make_async_copy(r_ref, rv, loc_sem.at[1])
    r_in.start()
    k_in = pltpu.make_async_copy(k_ref, kv, loc_sem.at[2])
    k_in.start()
    t_in.wait()
    for n in range(nodes):
        tw[n, rows_of(c), :] = jnp.where(row_at < ranks_ref[n], tv[n], 0.0)
    pl.semaphore_wait(barrier, 3)

    sent = []

    def copy(kind, n, src, dst, device):
        return pltpu.make_async_remote_copy(
            src_ref=src, dst_ref=dst, send_sem=send_sem.at[kind, n], recv_sem=recv_sem.at[kind, n],
            device_id=device, device_id_type=MESH,
        )

    def send(kind, n, src, dst, device):
        one = copy(kind, n, src, dst, device)
        one.start()
        sent.append(one)

    def got(kind, n, ref, device):
        copy(kind, n, ref, ref, device).wait_recv()

    def slot(n, s):
        return lv.at[n, pl.ds(s * block, block)]

    def strip(buf, n, index):
        return buf.at[n, rows_of(index)]

    half = 3 * block // 4
    rest = block - half
    last = nodes - 1

    def piece(n, s, first):
        return lv.at[n, pl.ds(s * block + first, rest if first else half)]

    def send_basis(n):
        send(LY, n, l_ref.at[n], slot(n, 2), to_y)

    for n in range(nodes):
        send(TY, n, strip(tw, n, c), strip(tw, n, c), to_y)
        send(TZ, n, strip(tw, n, c), strip(zw, n, c), to_z)
        send(TC, n, strip(tw, n, c), strip(tw, n, c), to_core)
    for n in range(nodes):
        if n < last:
            send_basis(n)
        send(LC, n, l_ref.at[n], slot(n, 1), to_core)
    def times(n, first, size):
        span = pl.ds(first, size)
        return jnp.dot(dv[n, :, span], lv[n, span, :], preferred_element_type=jnp.float32)

    def relay(n):
        got(TY, n, strip(tw, n, yp), to_y)
        send(TG, n, strip(tw, n, yp), strip(zw, n, yp), to_z)
        send(TF, n, strip(tw, n, yp), strip(tw, n, yp), to_core)

    def begin(n):
        l_in[n].wait()
        for s in range(4):
            d_in[4 * n + s].wait()
        got(LC, n, slot(n, 1), to_core)
        return times(n, 0, 2 * block)

    def eliminate(n):
        total = begin(n)
        got(LY, n, slot(n, 2), to_y)
        send(LF, n, slot(n, 2), slot(n, 3), to_core)
        total = total + times(n, 2 * block, block)
        got(LF, n, slot(n, 3), to_core)
        total = total + times(n, 3 * block, block)
        skeletons(n, total)

    def skeletons(n, total):
        skeleton = lax.dot_general(
            rv[n], total.astype(jnp.bfloat16), (((0,), (0,)), ((), ())), preferred_element_type=jnp.float32
        )
        sbuf[n] = skeleton.reshape(2, 2, part, width)
        send(SC, n, sbuf.at[n, :, 1 - core], sgot.at[n], to_core)

    def reduce_chip(n):
        got(SC, n, sgot.at[n], to_core)
        ysend[n] = (sbuf[n, other, core] + sgot[n, other]).astype(ysend.dtype)
        send(SY, n, ysend.at[n], ygot.at[n], to_y)

    def couple(n):
        got(ZC, n, strip(zw, n, cp), to_core)
        got(ZG, n, strip(zw, n, slots[3]), to_core)
        got(TC, n, strip(tw, n, cp), to_core)
        got(TF, n, strip(tw, n, slots[3]), to_core)
        mv[n] = product(kv[n], zw[n], (1, 0))

    outs = []

    def merge(n):
        got(SY, n, ygot.at[n], to_y)
        mine = sbuf[n, y, core] + sgot[n, y] + ygot[n].astype(jnp.float32)
        live = (row_at < ranks_ref[n]) & (col_at < ranks_ref[n])
        mine = jnp.where(live, mine, 0.0)
        merged = mv[n] + product(mine, tw[n], (1, 0))
        mv[n] = merged
        own = product(tw[n, rows_of(c), :], merged, (0, 0))
        pbuf[n] = own.reshape(2, 2, part, width)
        send(PC, n, pbuf.at[n, :, 1 - core], pgot.at[n], to_core)
        one = pltpu.make_async_copy(mv.at[n], out_ref.at[0, n], out_sem.at[0, n])
        one.start()
        outs.append(one)

    def parent_chip(n):
        got(PC, n, pgot.at[n], to_core)
        over = pbuf[n, other, core] + pgot[n, other]
        if n < last:
            pysend[n] = over
            send(PY, n, pysend.at[n], pygot.at[n], to_y)
        else:
            qsend[...] = over.astype(qsend.dtype)
            send(PY, n, qsend, qgot, to_y)

    def parent_own(n):
        if n < last:
            got(PY, n, pygot.at[n], to_y)
            came = pygot[n]
        else:
            got(PY, n, qgot, to_y)
            came = qgot[...].astype(jnp.float32)
        own = pbuf[n, y, core] + pgot[n, y] + came
        pv[n] = own
        esend[n] = own.astype(esend.dtype)
        send(PZ, n, esend.at[n], egot.at[n], to_z)

    def parent_all(n):
        got(PZ, n, egot.at[n], to_z)
        pv[n] = pv[n] + egot[n].astype(jnp.float32)
        one = pltpu.make_async_copy(pv.at[n], out_ref.at[1, n], out_sem.at[1, n])
        one.start()
        outs.append(one)

    r_in.wait()
    k_in.wait()
    for n in range(nodes):
        relay(n)
    eliminate(0)
    reduce_chip(0)
    send(LY, last, l_ref.at[last, pl.ds(0, half)], piece(last, 2, 0), to_y)
    for n in range(nodes):
        got(TZ, n, strip(zw, n, c), to_z)
        send(ZC, n, strip(zw, n, c), strip(zw, n, c), to_core)
    for n in range(1, last):
        eliminate(n)
        reduce_chip(n)
    send(MY, last, l_ref.at[last, pl.ds(half, rest)], piece(last, 2, half), to_y)

    def hand_on(n):
        got(TG, n, strip(zw, n, yp), to_z)
        send(ZG, n, strip(zw, n, yp), strip(zw, n, yp), to_core)

    hand_on(0)
    couple(0)
    merge(0)
    total = begin(last)
    parent_chip(0)
    got(LY, last, piece(last, 2, 0), to_y)
    send(LF, last, piece(last, 2, 0), piece(last, 3, 0), to_core)
    total = total + times(last, 2 * block, half)
    for n in range(1, last):
        hand_on(n)
    got(LF, last, piece(last, 3, 0), to_core)
    total = total + times(last, 3 * block, half)
    got(MY, last, piece(last, 2, half), to_y)
    send(MF, last, piece(last, 2, half), piece(last, 3, half), to_core)
    total = total + times(last, 2 * block + half, rest)
    for n in range(1, last):
        couple(n)
    got(MF, last, piece(last, 3, half), to_core)
    total = total + times(last, 3 * block + half, rest)
    skeletons(last, total)
    for n in range(1, last):
        merge(n)
    reduce_chip(last)
    for n in range(1, last):
        parent_chip(n)
    parent_own(0)
    hand_on(last)
    couple(last)
    merge(last)
    for n in range(1, last):
        parent_own(n)
    parent_chip(last)
    parent_all(0)
    parent_own(last)
    for n in range(1, last):
        parent_all(n)
    parent_all(last)
    for one in sent:
        one.wait_send()
    for one in outs:
        one.wait()


def shards(diagonal_inverses, column_basis, row_basis, transfer, coupling, ranks):
    nodes, block, whole = diagonal_inverses.shape
    part, width = transfer.shape[1:]
    f32, bf16 = jnp.float32, jnp.bfloat16
    skeleton_link, parent_link, sibling_link = bf16, f32, bf16
    anywhere = pl.BlockSpec(memory_space=pl.ANY)
    strips = (nodes, part, width)
    square = (nodes, width, width)
    quads = (nodes, 2, 2, part, width)
    pairs = (nodes, 2, part, width)
    out = pl.pallas_call(
        kernel,
        out_shape=jax.ShapeDtypeStruct((2,) + strips, f32),
        in_specs=[pl.BlockSpec(memory_space=pltpu.SMEM)] + [anywhere] * 5,
        out_specs=anywhere,
        scratch_shapes=[
            pltpu.VMEM((nodes, block, whole), bf16),
            pltpu.VMEM((nodes, whole, width), bf16),
            pltpu.VMEM((nodes, block, width), bf16),
            pltpu.VMEM(strips, f32),
            pltpu.VMEM(strips, f32),
            pltpu.VMEM(square, f32),
            pltpu.VMEM(square, f32),
            pltpu.VMEM(quads, f32),
            pltpu.VMEM(pairs, f32),
            pltpu.VMEM(strips, skeleton_link),
            pltpu.VMEM(strips, skeleton_link),
            pltpu.VMEM(quads, f32),
            pltpu.VMEM(pairs, f32),
            pltpu.VMEM(strips, parent_link),
            pltpu.VMEM(strips, parent_link),
            pltpu.VMEM((part, width), bf16),
            pltpu.VMEM((part, width), bf16),
            pltpu.VMEM(strips, sibling_link),
            pltpu.VMEM(strips, sibling_link),
            pltpu.VMEM(strips, f32),
            pltpu.VMEM(strips, f32),
            pltpu.SemaphoreType.DMA((17, nodes)),
            pltpu.SemaphoreType.DMA((17, nodes)),
            pltpu.SemaphoreType.DMA((nodes, 5)),
            pltpu.SemaphoreType.DMA((3,)),
            pltpu.SemaphoreType.DMA((2, nodes)),
        ],
        compiler_params=pltpu.CompilerParams(collective_id=0, has_side_effects=True),
    )(ranks, diagonal_inverses, column_basis, row_basis, transfer, coupling)
    return out[0], out[1]


def solution(mesh):
    placed = (P("row", "col", None),) * 5 + (P("row"),)
    return jax.shard_map(
        shards,
        mesh=mesh,
        in_specs=placed,
        out_specs=(P("row", "col", None), P("row", "col", None)),
        check_vma=False,
    )
```

```python
import jax
import jax.numpy as jnp
from jax import lax
from jax.experimental import pallas as pl
from jax.experimental.pallas import tpu as pltpu
from jax.sharding import PartitionSpec as P

BIT = 2
MESH = pl.DeviceIdType.MESH
LY, LC, LF, TY, TC, TF, TZ, TG, ZC, ZG, SC, SY, PC, PY, PZ, MY, MF = range(17)


def kernel(
    ranks_ref, d_ref, l_ref, r_ref, t_ref, k_ref, out_ref,
    dv, lv, rv, tv, kv, tw, zw, sbuf, sgot, ysend, ygot, pbuf, pgot, pysend, pygot, qsend, qgot,
    esend, egot, mv, pv, send_sem, recv_sem, d_sem, loc_sem, out_sem,
):
    nodes, block, _ = l_ref.shape
    part = t_ref.shape[1]
    width = t_ref.shape[2]
    c = lax.axis_index("col")
    r = lax.axis_index("row")
    core = lax.rem(c, 2)
    y = lax.div(c, 2)
    cp = c + 1 - 2 * core
    yp = c + 2 - 4 * y
    high = lax.rem(lax.div(r, 1 << BIT), 2)
    sib = r + (1 << BIT) - (2 << BIT) * high
    other = 1 - y

    to_core = {"col": cp}
    to_y = {"col": yp}
    to_z = {"row": sib}
    slots = (c, cp, yp, cp + yp - c)

    def halves(x):
        top = x.astype(jnp.bfloat16)
        return top, (x - top.astype(jnp.float32)).astype(jnp.bfloat16)

    def product(a, b, dims):
        a_top, a_low = halves(a)
        b_top, b_low = halves(b)
        lhs = jnp.concatenate([a_top, a_low, a_top], axis=dims[0])
        rhs = jnp.concatenate([b_top, b_top, b_low], axis=dims[1])
        return lax.dot_general(
            lhs, rhs, (((dims[0],), (dims[1],)), ((), ())), preferred_element_type=jnp.float32
        )

    def rows_of(index):
        return pl.ds(pl.multiple_of(index * part, part), part)

    t_in = pltpu.make_async_copy(t_ref, tv, loc_sem.at[0])
    t_in.start()
    barrier = pltpu.get_barrier_semaphore()
    for device in (to_core, to_y, to_z):
        pl.semaphore_signal(barrier, inc=1, device_id=device, device_id_type=MESH)

    row_at = lax.broadcasted_iota(jnp.int32, (part, width), 0) + c * part
    col_at = lax.broadcasted_iota(jnp.int32, (part, width), 1)
    l_in, d_in = [], []
    for n in range(nodes):
        cp_l = pltpu.make_async_copy(l_ref.at[n], lv.at[n, pl.ds(0, block)], d_sem.at[n, 4])
        cp_l.start()
        l_in.append(cp_l)
        for s in range(4):
            src = d_ref.at[n, :, pl.ds(pl.multiple_of(slots[s] * block, block), block)]
            one = pltpu.make_async_copy(src, dv.at[n, :, pl.ds(s * block, block)], d_sem.at[n, s])
            one.start()
            d_in.append(one)
    r_in = pltpu.make_async_copy(r_ref, rv, loc_sem.at[1])
    r_in.start()
    k_in = pltpu.make_async_copy(k_ref, kv, loc_sem.at[2])
    k_in.start()
    t_in.wait()
    for n in range(nodes):
        tw[n, rows_of(c), :] = jnp.where(row_at < ranks_ref[n], tv[n], 0.0)
    pl.semaphore_wait(barrier, 3)

    sent = []

    def copy(kind, n, src, dst, device):
        return pltpu.make_async_remote_copy(
            src_ref=src, dst_ref=dst, send_sem=send_sem.at[kind, n], recv_sem=recv_sem.at[kind, n],
            device_id=device, device_id_type=MESH,
        )

    def send(kind, n, src, dst, device):
        one = copy(kind, n, src, dst, device)
        one.start()
        sent.append(one)

    def got(kind, n, ref, device):
        copy(kind, n, ref, ref, device).wait_recv()

    def slot(n, s):
        return lv.at[n, pl.ds(s * block, block)]

    def strip(buf, n, index):
        return buf.at[n, rows_of(index)]

    half = block // 2
    rest = block - half
    last = nodes - 1

    def piece(n, s, first):
        return lv.at[n, pl.ds(s * block + first, rest if first else half)]

    def send_basis(n):
        send(LY, n, l_ref.at[n], slot(n, 2), to_y)

    for n in range(nodes):
        send(TY, n, strip(tw, n, c), strip(tw, n, c), to_y)
        send(TZ, n, strip(tw, n, c), strip(zw, n, c), to_z)
        send(TC, n, strip(tw, n, c), strip(tw, n, c), to_core)
    for n in range(nodes):
        if n < last:
            send_basis(n)
        send(LC, n, l_ref.at[n], slot(n, 1), to_core)
    def times(n, first, size):
        span = pl.ds(first, size)
        return jnp.dot(dv[n, :, span], lv[n, span, :], preferred_element_type=jnp.float32)

    def relay(n):
        got(TY, n, strip(tw, n, yp), to_y)
        send(TG, n, strip(tw, n, yp), strip(zw, n, yp), to_z)
        send(TF, n, strip(tw, n, yp), strip(tw, n, yp), to_core)

    def begin(n):
        l_in[n].wait()
        for s in range(4):
            d_in[4 * n + s].wait()
        got(LC, n, slot(n, 1), to_core)
        return times(n, 0, 2 * block)

    def eliminate(n):
        total = begin(n)
        got(LY, n, slot(n, 2), to_y)
        send(LF, n, slot(n, 2), slot(n, 3), to_core)
        total = total + times(n, 2 * block, block)
        got(LF, n, slot(n, 3), to_core)
        total = total + times(n, 3 * block, block)
        skeletons(n, total)

    def skeletons(n, total):
        skeleton = lax.dot_general(
            rv[n], total.astype(jnp.bfloat16), (((0,), (0,)), ((), ())), preferred_element_type=jnp.float32
        )
        sbuf[n] = skeleton.reshape(2, 2, part, width)
        send(SC, n, sbuf.at[n, :, 1 - core], sgot.at[n], to_core)

    def reduce_chip(n):
        got(SC, n, sgot.at[n], to_core)
        ysend[n] = (sbuf[n, other, core] + sgot[n, other]).astype(ysend.dtype)
        send(SY, n, ysend.at[n], ygot.at[n], to_y)

    def couple(n):
        got(ZC, n, strip(zw, n, cp), to_core)
        got(ZG, n, strip(zw, n, slots[3]), to_core)
        got(TC, n, strip(tw, n, cp), to_core)
        got(TF, n, strip(tw, n, slots[3]), to_core)
        mv[n] = product(kv[n], zw[n], (1, 0))

    outs = []

    def merge(n):
        got(SY, n, ygot.at[n], to_y)
        mine = sbuf[n, y, core] + sgot[n, y] + ygot[n].astype(jnp.float32)
        live = (row_at < ranks_ref[n]) & (col_at < ranks_ref[n])
        mine = jnp.where(live, mine, 0.0)
        merged = mv[n] + product(mine, tw[n], (1, 0))
        mv[n] = merged
        own = product(tw[n, rows_of(c), :], merged, (0, 0))
        pbuf[n] = own.reshape(2, 2, part, width)
        send(PC, n, pbuf.at[n, :, 1 - core], pgot.at[n], to_core)
        one = pltpu.make_async_copy(mv.at[n], out_ref.at[0, n], out_sem.at[0, n])
        one.start()
        outs.append(one)

    def parent_chip(n):
        got(PC, n, pgot.at[n], to_core)
        over = pbuf[n, other, core] + pgot[n, other]
        if n < last:
            pysend[n] = over
            send(PY, n, pysend.at[n], pygot.at[n], to_y)
        else:
            qsend[...] = over.astype(qsend.dtype)
            send(PY, n, qsend, qgot, to_y)

    def parent_own(n):
        if n < last:
            got(PY, n, pygot.at[n], to_y)
            came = pygot[n]
        else:
            got(PY, n, qgot, to_y)
            came = qgot[...].astype(jnp.float32)
        own = pbuf[n, y, core] + pgot[n, y] + came
        pv[n] = own
        esend[n] = own.astype(esend.dtype)
        send(PZ, n, esend.at[n], egot.at[n], to_z)

    def parent_all(n):
        got(PZ, n, egot.at[n], to_z)
        pv[n] = pv[n] + egot[n].astype(jnp.float32)
        one = pltpu.make_async_copy(pv.at[n], out_ref.at[1, n], out_sem.at[1, n])
        one.start()
        outs.append(one)

    r_in.wait()
    k_in.wait()
    for n in range(nodes):
        relay(n)
    eliminate(0)
    reduce_chip(0)
    send(LY, last, l_ref.at[last, pl.ds(0, half)], piece(last, 2, 0), to_y)
    send(MY, last, l_ref.at[last, pl.ds(half, rest)], piece(last, 2, half), to_y)
    for n in range(nodes):
        got(TZ, n, strip(zw, n, c), to_z)
        send(ZC, n, strip(zw, n, c), strip(zw, n, c), to_core)
    for n in range(1, last):
        eliminate(n)
        reduce_chip(n)

    def hand_on(n):
        got(TG, n, strip(zw, n, yp), to_z)
        send(ZG, n, strip(zw, n, yp), strip(zw, n, yp), to_core)

    hand_on(0)
    couple(0)
    merge(0)
    total = begin(last)
    parent_chip(0)
    got(LY, last, piece(last, 2, 0), to_y)
    send(LF, last, piece(last, 2, 0), piece(last, 3, 0), to_core)
    total = total + times(last, 2 * block, half)
    for n in range(1, last):
        hand_on(n)
    got(LF, last, piece(last, 3, 0), to_core)
    total = total + times(last, 3 * block, half)
    got(MY, last, piece(last, 2, half), to_y)
    send(MF, last, piece(last, 2, half), piece(last, 3, half), to_core)
    total = total + times(last, 2 * block + half, rest)
    for n in range(1, last):
        couple(n)
    got(MF, last, piece(last, 3, half), to_core)
    total = total + times(last, 3 * block + half, rest)
    skeletons(last, total)
    for n in range(1, last):
        merge(n)
    reduce_chip(last)
    for n in range(1, last):
        parent_chip(n)
    parent_own(0)
    hand_on(last)
    couple(last)
    merge(last)
    for n in range(1, last):
        parent_own(n)
    parent_chip(last)
    parent_all(0)
    parent_own(last)
    for n in range(1, last):
        parent_all(n)
    parent_all(last)
    for one in sent:
        one.wait_send()
    for one in outs:
        one.wait()


def shards(diagonal_inverses, column_basis, row_basis, transfer, coupling, ranks):
    nodes, block, whole = diagonal_inverses.shape
    part, width = transfer.shape[1:]
    f32, bf16 = jnp.float32, jnp.bfloat16
    skeleton_link, parent_link, sibling_link = bf16, f32, bf16
    anywhere = pl.BlockSpec(memory_space=pl.ANY)
    strips = (nodes, part, width)
    square = (nodes, width, width)
    quads = (nodes, 2, 2, part, width)
    pairs = (nodes, 2, part, width)
    out = pl.pallas_call(
        kernel,
        out_shape=jax.ShapeDtypeStruct((2,) + strips, f32),
        in_specs=[pl.BlockSpec(memory_space=pltpu.SMEM)] + [anywhere] * 5,
        out_specs=anywhere,
        scratch_shapes=[
            pltpu.VMEM((nodes, block, whole), bf16),
            pltpu.VMEM((nodes, whole, width), bf16),
            pltpu.VMEM((nodes, block, width), bf16),
            pltpu.VMEM(strips, f32),
            pltpu.VMEM(strips, f32),
            pltpu.VMEM(square, f32),
            pltpu.VMEM(square, f32),
            pltpu.VMEM(quads, f32),
            pltpu.VMEM(pairs, f32),
            pltpu.VMEM(strips, skeleton_link),
            pltpu.VMEM(strips, skeleton_link),
            pltpu.VMEM(quads, f32),
            pltpu.VMEM(pairs, f32),
            pltpu.VMEM(strips, parent_link),
            pltpu.VMEM(strips, parent_link),
            pltpu.VMEM((part, width), bf16),
            pltpu.VMEM((part, width), bf16),
            pltpu.VMEM(strips, sibling_link),
            pltpu.VMEM(strips, sibling_link),
            pltpu.VMEM(strips, f32),
            pltpu.VMEM(strips, f32),
            pltpu.SemaphoreType.DMA((17, nodes)),
            pltpu.SemaphoreType.DMA((17, nodes)),
            pltpu.SemaphoreType.DMA((nodes, 5)),
            pltpu.SemaphoreType.DMA((3,)),
            pltpu.SemaphoreType.DMA((2, nodes)),
        ],
        compiler_params=pltpu.CompilerParams(collective_id=0, has_side_effects=True),
    )(ranks, diagonal_inverses, column_basis, row_basis, transfer, coupling)
    return out[0], out[1]


def solution(mesh):
    placed = (P("row", "col", None),) * 5 + (P("row"),)
    return jax.shard_map(
        shards,
        mesh=mesh,
        in_specs=placed,
        out_specs=(P("row", "col", None), P("row", "col", None)),
        check_vma=False,
    )
```
